32 devices in a mesh: mid: 16 (over z, y, x), fin: 2 (over core).
Axes of the slice: x: 2, y: 2, z: 4, core: 2. Of those that a mesh axis runs over, the one named last changes fastest.
Arguments:
- history: float32 [256, 16, 64, 128], P('mid', 'fin'), may hold values from -6 to 6
- sigma: float32 [4, 256, 64, 128], P(None, 'mid', 'fin'), may hold values from -0.0234375 to 0.0234375
- propagator: float32 [64, 128], replicated, may hold values from -0.375 to 0.375
Outputs:
- new_rows: float32 [4, 16, 64, 128], P(None, 'fin', 'mid')
The draws below stay inside these ranges and needn't reach their ends.
All inputs are finite; a program needn't handle non-finite values.
Results may differ from the reference program's by a relative error of at most 0.0003.
Values sent between devices are 32-bit elements; how exact they have to be, the bound alone decides.
A program may use at most 128 MiB of HBM per device.

```python
import jax
import jax.numpy as jnp
from jax import lax

NO = 64
COLS_DEV = 8
STEPS = 4
H = 256
NCOL = 16


def block_scale(stream_key, dims, split, least, high):
    gain, own = 1.0, jax.random.fold_in(stream_key, 6)
    for dim, blocks in split:
        steps = jnp.exp(jax.random.uniform(jax.random.fold_in(own, dim), (blocks,), jnp.float32, least / len(split), high / len(split)))
        gain = gain * jnp.repeat(steps, dims[dim] // blocks).reshape([-1 if axis == dim else 1 for axis in range(len(dims))])
    return gain


def noise(stream_key, extent, spread, most, pieces=(), kind=jnp.bfloat16):
    gain = block_scale(stream_key, extent, pieces, -0.22, 0.18) if pieces else 1.0
    entries = jax.random.normal(stream_key, extent, jnp.float32) * spread * gain
    return jnp.minimum(jnp.maximum(entries, -most), most).astype(kind)


def setup_inputs(seed: int = 0) -> dict:
    arg_keys = jax.random.split(jax.random.key(seed), 4)
    return {
        "history": noise(arg_keys[0], (H, NCOL, NO, 2 * NO), 1.0, 6.0, ((0, 16), (1, 2)), jnp.float32),
        "sigma": noise(arg_keys[1], (STEPS, H, NO, 2 * NO), (4 * NO * H) ** -0.5, 0.0234375, ((1, 16), (2, 2)), jnp.float32),
        "propagator": noise(arg_keys[2], (NO, 2 * NO), (4 * NO) ** -0.5, 0.375, (), jnp.float32),
    }


def turn_pair(block, axis):
    half = block.shape[-1] // 2
    turned = jnp.concatenate([-block[..., half:], block[..., :half]], axis=-1)
    return jnp.concatenate([block, turned], axis=axis)


def integral(kernel, block, keep):
    masked = block * keep[:, :, None, None]
    stacked = turn_pair(masked, 2)
    return jnp.einsum('sik,sckj->cij', kernel, stacked, precision=lax.Precision.HIGHEST)


def propagate(weight, latest):
    stacked = turn_pair(latest, 1)
    return jnp.einsum('ik,ckj->cij', weight, stacked, precision=lax.Precision.HIGHEST)


def reference(history, sigma, propagator):
    ncol = history.shape[1]
    width = history.shape[0]
    col_times = (jnp.arange(ncol, dtype=jnp.int32) * width) // ncol
    slots = jnp.arange(width, dtype=jnp.int32)
    state = history
    latest = history[width - 1]
    outputs = []
    groups = ncol // COLS_DEV
    for step in range(STEPS):
        slot_times = jnp.where(slots >= step, slots, slots + width)
        keep = (slot_times[:, None] >= col_times[None, :]).astype(jnp.float32)
        kernel = sigma[step]

        def block_terms(group):
            start = (group * COLS_DEV).astype(jnp.int32)
            block = lax.dynamic_slice_in_dim(state, start, COLS_DEV, 1)
            keep_block = lax.dynamic_slice_in_dim(keep, start, COLS_DEV, 1)
            return integral(kernel, block, keep_block)

        memory = lax.map(block_terms, jnp.arange(groups, dtype=jnp.int32))
        memory = memory.reshape(ncol, history.shape[2], history.shape[3])
        new_row = propagate(propagator, latest) + memory
        state = state.at[step].set(new_row)
        latest = new_row
        outputs.append(new_row)
    return jnp.stack(outputs)
```

```python
import functools

import jax
import jax.numpy as jnp
from jax import lax
from jax.experimental import pallas as pl
from jax.experimental.pallas import tpu as pltpu
from jax.sharding import PartitionSpec as P

MESH = pl.DeviceIdType.MESH
PLANE = 4
F32 = jnp.float32
BF16 = jnp.bfloat16


def split(value):
    high = value.astype(BF16)
    return high, (value - high.astype(F32)).astype(BF16)


def turn(value):
    half = value.shape[-1] // 2
    rolled = pltpu.roll(value, half, 1)
    lane = lax.broadcasted_iota(jnp.int32, value.shape, 1)
    return jnp.where(lane < half, -rolled, rolled)


def stack(value):
    return jnp.concatenate([value, turn(value)], axis=0)


def kernel(
    n, f, hist_ref, sigma_ref, prop_hbm, outb,
    hist, sig, prop_ref, sbuf, lhs, rhs, part, rx1, rx2, weights, stage, zeros,
    hist_sem, prop_sem, sig_local, sig_send, sig_recv, s_local, s_send, s_recv,
    sx_send, sx_recv, greet, x1_send, x1_recv, x2_send, x2_recv, o_send, o_recv,
):
    m = lax.axis_index("mid")
    q = lax.axis_index("fin")
    slots, cols, rows, lanes = hist_ref.shape
    steps, rf = sigma_ref.shape[0], sigma_ref.shape[2]
    width, ncol = n * slots, f * cols
    planes, groups = n // PLANE, cols // PLANE
    rc = rows // n
    half = lanes // 2
    depth = slots * half
    x, y, z = m % 2, (m // 2) % 2, m // PLANE
    xy = m % PLANE
    base = m - xy
    o = q % 2
    b1, b2 = x + o * (y - x), y + o * (x - y)
    w1, w2 = 1 + o, 2 - o
    partner1, partner2 = m + w1 * (1 - 2 * b1), m + w2 * (1 - 2 * b2)

    def remote(src, dst, send, recv, **where):
        return pltpu.make_async_remote_copy(
            src_ref=src, dst_ref=dst, send_sem=send, recv_sem=recv,
            device_id=where, device_id_type=MESH,
        )

    def tell(sem, **where):
        pl.semaphore_signal(sem, inc=1, device_id=where, device_id_type=MESH)

    def mate(d):
        return base + (xy + d) % PLANE

    def col_time(local, fin):
        return ((fin * cols + local) * width) // ncol

    def active(plane, g):
        return (plane * PLANE + PLANE) * slots - 1 >= col_time(g * PLANE, q)

    def column(g, flip1, flip2):
        c1 = 1 - b1 if flip1 else b1
        c2 = 1 - b2 if flip2 else b2
        return g * PLANE + c1 * w1 + c2 * w2

    order = []
    for flip1 in (True, False):
        for g in range(groups):
            order.append((column(g, flip1, True), column(g, flip1, False)))

    own_sigma = pltpu.make_async_copy(sigma_ref, sig.at[q], sig_local)
    own_sigma.start()
    own_prop = pltpu.make_async_copy(prop_hbm, prop_ref, prop_sem)
    own_prop.start()

    barrier = pltpu.get_barrier_semaphore()
    for d in range(1, f):
        tell(barrier, fin=(q + d) % f)
    for d in range(1, PLANE):
        tell(barrier, mid=mate(d))
    for p in range(1, planes):
        @pl.when(z < p)
        def _():
            tell(barrier, mid=p * PLANE + xy)

    def s_copies():
        return [
            pltpu.make_async_copy(
                sigma_ref.at[k, pl.ds(0, k)],
                sbuf.at[q, pl.ds(k * (k - 1) // 2, k)],
                s_local.at[k - 1],
            )
            for k in range(1, steps)
        ]

    @pl.when(m == 0)
    def _():
        for copy in s_copies():
            copy.start()

    loads = []
    for i, pair in enumerate(order):
        for j, c in enumerate(pair):
            copy = pltpu.make_async_copy(
                hist_ref.at[:, c], hist.at[c], hist_sem.at[2 * i + j]
            )
            copy.start()
            loads.append(copy)

    zeros[...] = jnp.zeros_like(zeros)
    for g in range(groups):
        for p in range(planes):
            @pl.when(jnp.logical_not(active(p, g)))
            def _():
                pltpu.make_async_copy(zeros, outb.at[g, p], o_recv.at[g, p]).start()

    def build(fq):
        lane = lax.broadcasted_iota(jnp.int32, (rf, lanes), 1)
        is_last = (m == n - 1).astype(F32)
        for k in range(steps):
            for t in range(slots // 2):
                a, b = sig[fq, k, 2 * t], sig[fq, k, 2 * t + 1]
                if 2 * t < k:
                    a = a * (m * slots + 2 * t >= k).astype(F32)
                if 2 * t + 1 < k:
                    b = b * (m * slots + 2 * t + 1 >= k).astype(F32)
                if k == 0 and 2 * t + 2 == slots:
                    b = b + prop_ref[pl.ds(pl.multiple_of(fq * rf, rf), rf)] * is_last
                real = jnp.where(lane < half, a, pltpu.roll(b, half, 1))
                imag = jnp.where(lane < half, pltpu.roll(a, half, 1), b)
                for part_id, value in enumerate((real, imag)):
                    row = (part_id * steps + k) * rf
                    high, low = split(value)
                    lhs[fq, row:row + rf, t * lanes:(t + 1) * lanes] = high
                    lhs[fq, row:row + rf, depth + t * lanes:depth + (t + 1) * lanes] = low

    own_sigma.wait()
    own_prop.wait()
    build(q)
    pl.semaphore_wait(barrier, f - 1 + PLANE - 1 + z)

    sig_out = []
    for d in range(1, f):
        copy = remote(sigma_ref, sig.at[q], sig_send.at[d], sig_recv.at[q], fin=(q + d) % f)
        copy.start()
        sig_out.append(copy)

    for d in range(1, PLANE):
        tell(greet, mid=mate(d))
    for p in range(planes - 1):
        @pl.when(z > p)
        def _():
            tell(greet, mid=p * PLANE + xy)

    def s_first(to):
        return remote(sbuf.at[q], sbuf.at[q], s_send.at[to], s_recv, mid=to)

    def s_second(p):
        return remote(sbuf.at[q], sbuf.at[q], s_send.at[PLANE + p], s_recv, mid=p * PLANE + xy)

    firsts = (2, 3, 1)

    @pl.when(m == 0)
    def _():
        for copy in s_copies():
            copy.wait()
        for to in firsts:
            s_first(to).start()

    def prepare(i):
        for j, c in enumerate(order[i]):
            loads[2 * i + j].wait()

        @pl.when(active(z, i % groups))
        def _():
            for j, c in enumerate(order[i]):
                start = col_time(c, q)
                for s in range(slots):
                    keep = (m * slots + s >= start).astype(F32)
                    high, low = split(hist[c, s] * keep)
                    rhs[i, s * half:(s + 1) * half, j * lanes:(j + 1) * lanes] = high
                    rhs[i, depth + s * half:depth + (s + 1) * half, j * lanes:(j + 1) * lanes] = low

    def compute(i, fq):
        dot = functools.partial(jnp.dot, preferred_element_type=F32)
        total = dot(lhs[fq, :, :depth], rhs[i, :depth])
        total = total + dot(lhs[fq, :, :depth], rhs[i, depth:])
        total = total + dot(lhs[fq, :, depth:], rhs[i, :depth])
        many = steps * rf
        for j, c in enumerate(order[i]):
            block = total[:, j * lanes:(j + 1) * lanes]
            part[c, fq] = block[:many] + turn(block[many:])

    def x1_copy(g, j, fq):
        return remote(
            part.at[order[g][j], fq], rx1.at[g, j, fq],
            x1_send.at[g, j, fq], x1_recv.at[g, j, fq], mid=partner1,
        )

    def x2_copy(g, fq):
        return remote(
            part.at[order[groups + g][0], fq], rx2.at[g, fq],
            x2_send.at[g, fq], x2_recv.at[g, fq], mid=partner2,
        )

    def send(g, fq):
        @pl.when(active(z, g))
        def _():
            compute(g, fq)
            for j in range(2):
                x1_copy(g, j, fq).start()

    def hold(g, fq):
        @pl.when(active(z, g))
        def _():
            compute(groups + g, fq)

    def forward(g, fq):
        @pl.when(active(z, g))
        def _():
            c = order[groups + g][0]
            x1_copy(g, 0, fq).wait_recv()
            part[c, fq] = part[c, fq] + rx1[g, 0, fq]
            x2_copy(g, fq).start()

    for g in range(groups):
        prepare(g)
        send(g, q)
    others = [(q + r) % f for r in range(1, f)]
    for r, fq in enumerate(others):
        remote(sigma_ref, sig.at[fq], sig_send.at[1 + r], sig_recv.at[fq], fin=fq).wait_recv()
        build(fq)
        for g in range(groups):
            send(g, fq)

    pl.semaphore_wait(greet, PLANE - 1 + planes - 1 - z)

    @pl.when(z == 0)
    def _():
        @pl.when(m != 0)
        def _():
            s_first(0).wait_recv()
        for p in reversed(range(1, planes)):
            s_second(p).start()

    for g in range(groups):
        prepare(groups + g)
        for fq in (q, *others):
            hold(g, fq)
        for fq in (q, *others):
            forward(g, fq)

    @pl.when(z != 0)
    def _():
        s_second(0).wait_recv()

    sx_out = []
    for d in range(1, f):
        copy = remote(sbuf.at[q], sbuf.at[q], sx_send.at[d], sx_recv.at[q], fin=(q + d) % f)
        copy.start()
        sx_out.append(copy)
    for fq in others:
        remote(sbuf.at[fq], sbuf.at[fq], sx_send.at[0], sx_recv.at[fq], fin=fq).wait_recv()

    exact = functools.partial(
        jnp.dot, preferred_element_type=F32, precision=lax.Precision.HIGHEST
    )
    direct, whole = {}, {}
    for k in range(1, steps):
        for j in range(k):
            pieces = [sbuf[fq, k * (k - 1) // 2 + j] for fq in range(f)]
            block = jnp.concatenate(pieces, axis=0)
            direct[k, j] = block + prop_ref[...] if k == j + 1 else block
    for k in range(1, steps):
        for j in range(steps - 1):
            block = direct[k, j] if j < k else jnp.zeros((rows, lanes), F32)
            for i in range(j + 1, k):
                block = block + exact(direct[k, i], stack(whole[i, j]))
            whole[k, j] = block
            high, low = split(block)
            weights[0, (k - 1) * rows:k * rows, j * lanes:(j + 1) * lanes] = high
            weights[1, (k - 1) * rows:k * rows, j * lanes:(j + 1) * lanes] = low

    def o_copy(g, to):
        return remote(stage.at[g, to], outb.at[g, z, xy], o_send.at[g], o_recv.at[g, z], mid=to)

    def finish(g):
        c = order[groups + g][1]
        row = []
        for fq in (q, *others):
            x1_copy(g, 1, fq).wait_recv()
            x2_copy(g, fq).wait_recv()
        for fq in range(f):
            part[c, fq] = part[c, fq] + rx1[g, 1, fq] + rx2[g, fq]
        for k in range(steps):
            pieces = [part[c, fq, k * rf:(k + 1) * rf] for fq in range(f)]
            row.append(jnp.concatenate(pieces, axis=0))
        high, low = split(jnp.concatenate([stack(row[k]) for k in range(steps - 1)], axis=0))
        dot = functools.partial(jnp.dot, preferred_element_type=F32)
        terms = dot(weights[0], high) + dot(weights[0], low) + dot(weights[1], high)
        for k in range(steps):
            value = row[k]
            if k > 0:
                value = value + terms[(k - 1) * rows:k * rows]
            for to in range(n):
                stage[g, to, k] = value[to * rc:(to + 1) * rc]
        for p in range(planes):
            for d in range(PLANE):
                to = p * PLANE + (xy + d) % PLANE
                if d:
                    o_copy(g, to).start()
                else:
                    @pl.when(p != z)
                    def _():
                        o_copy(g, to).start()
        pltpu.make_async_copy(stage.at[g, m], outb.at[g, z, xy], o_recv.at[g, z]).start()

    for g in range(groups):
        @pl.when(active(z, g))
        def _():
            finish(g)

    for g in range(groups):
        for p in range(planes):
            pltpu.make_async_copy(outb.at[g, p], outb.at[g, p], o_recv.at[g, p]).wait()

    for copy in sig_out + sx_out:
        copy.wait_send()

    @pl.when(m == 0)
    def _():
        for to in firsts:
            s_first(to).wait_send()

    @pl.when(z == 0)
    def _():
        for p in range(1, planes):
            s_second(p).wait_send()

    for g in range(groups):
        @pl.when(active(z, g))
        def _():
            for fq in range(f):
                x1_copy(g, 0, fq).wait_send()
                x1_copy(g, 1, fq).wait_send()
                x2_copy(g, fq).wait_send()
            sent = stage.at[g, pl.ds(0, n - 1)]
            pltpu.make_async_copy(sent, sent, o_send.at[g]).wait()


def solution(mesh):
    n, f = mesh.shape["mid"], mesh.shape["fin"]

    def on_device(history, sigma, propagator):
        slots, cols, rows, lanes = history.shape
        steps, rf = sigma.shape[0], sigma.shape[2]
        rc, depth = rows // n, slots * lanes // 2
        planes, groups, pairs = n // PLANE, cols // PLANE, steps * (steps - 1) // 2
        many = steps * rf
        dma = pltpu.SemaphoreType.DMA
        anywhere = pl.BlockSpec(memory_space=pl.ANY)
        out = pl.pallas_call(
            functools.partial(kernel, n, f),
            out_shape=jax.ShapeDtypeStruct((groups, planes, PLANE, steps, rc, lanes), F32),
            in_specs=[anywhere, anywhere, anywhere],
            out_specs=anywhere,
            scratch_shapes=[
                pltpu.VMEM((cols, slots, rows, lanes), F32),
                pltpu.VMEM((f, steps, slots, rf, lanes), F32),
                pltpu.VMEM((rows, lanes), F32),
                pltpu.VMEM((f, pairs, rf, lanes), F32),
                pltpu.VMEM((f, 2 * many, 2 * depth), BF16),
                pltpu.VMEM((2 * groups, 2 * depth, 2 * lanes), BF16),
                pltpu.VMEM((cols, f, many, lanes), F32),
                pltpu.VMEM((groups, 2, f, many, lanes), F32),
                pltpu.VMEM((groups, f, many, lanes), F32),
                pltpu.VMEM((2, (steps - 1) * rows, (steps - 1) * lanes), BF16),
                pltpu.VMEM((groups, n, steps, rc, lanes), F32),
                pltpu.VMEM((PLANE, steps, rc, lanes), F32),
                dma((cols,)), dma, dma, dma((f,)), dma((f,)),
                dma((steps - 1,)), dma((PLANE + planes,)), dma,
                dma((f,)), dma((f,)), pltpu.SemaphoreType.REGULAR,
                dma((groups, 2, f)), dma((groups, 2, f)), dma((groups, f)), dma((groups, f)),
                dma((groups,)), dma((groups, planes)),
            ],
            compiler_params=pltpu.CompilerParams(
                collective_id=0, has_side_effects=True, vmem_limit_bytes=60 * 2**20
            ),
        )(history, sigma, propagator)
        total = jnp.sum(out, axis=1).reshape(cols, steps, rc, lanes)
        return jnp.transpose(total, (1, 0, 2, 3))

    in_specs = (P("mid", "fin", None, None), P(None, "mid", "fin", None), P())
    return jax.shard_map(
        on_device, mesh=mesh, in_specs=in_specs, out_specs=P(None, "fin", "mid", None),
        check_vma=False,
    )
```

```python
import functools

import jax
import jax.numpy as jnp
from jax import lax
from jax.experimental import pallas as pl
from jax.experimental.pallas import tpu as pltpu
from jax.sharding import PartitionSpec as P

MESH = pl.DeviceIdType.MESH
PLANE = 4
F32 = jnp.float32
BF16 = jnp.bfloat16


def split(value):
    high = value.astype(BF16)
    return high, (value - high.astype(F32)).astype(BF16)


def turn(value):
    half = value.shape[-1] // 2
    rolled = pltpu.roll(value, half, 1)
    lane = lax.broadcasted_iota(jnp.int32, value.shape, 1)
    return jnp.where(lane < half, -rolled, rolled)


def stack(value):
    return jnp.concatenate([value, turn(value)], axis=0)


def kernel(
    n, f, hist_ref, sigma_ref, prop_hbm, outb,
    hist, sig, prop_ref, sbuf, lhs, rhs, part, rx1, rx2, weights, stage, zeros,
    hist_sem, prop_sem, sig_local, sig_send, sig_recv, s_local, s_send, s_recv,
    sx_send, sx_recv, greet, x1_send, x1_recv, x2_send, x2_recv, o_send, o_recv,
):
    m = lax.axis_index("mid")
    q = lax.axis_index("fin")
    slots, cols, rows, lanes = hist_ref.shape
    steps, rf = sigma_ref.shape[0], sigma_ref.shape[2]
    width, ncol = n * slots, f * cols
    planes, groups = n // PLANE, cols // PLANE
    rc = rows // n
    half = lanes // 2
    depth = slots * half
    x, y, z = m % 2, (m // 2) % 2, m // PLANE
    xy = m % PLANE
    base = m - xy
    o = (q + (z == 0).astype(jnp.int32)) % 2
    b1, b2 = x + o * (y - x), y + o * (x - y)
    w1, w2 = 1 + o, 2 - o
    partner1, partner2 = m + w1 * (1 - 2 * b1), m + w2 * (1 - 2 * b2)

    def remote(src, dst, send, recv, **where):
        return pltpu.make_async_remote_copy(
            src_ref=src, dst_ref=dst, send_sem=send, recv_sem=recv,
            device_id=where, device_id_type=MESH,
        )

    def tell(sem, **where):
        pl.semaphore_signal(sem, inc=1, device_id=where, device_id_type=MESH)

    def mate(d):
        return base + (xy + d) % PLANE

    def col_time(local, fin):
        return ((fin * cols + local) * width) // ncol

    def active(plane, g):
        return (plane * PLANE + PLANE) * slots - 1 >= col_time(g * PLANE, q)

    def column(g, flip1, flip2):
        c1 = 1 - b1 if flip1 else b1
        c2 = 1 - b2 if flip2 else b2
        return g * PLANE + c1 * w1 + c2 * w2

    order = []
    for flip1 in (True, False):
        for g in range(groups):
            order.append((column(g, flip1, True), column(g, flip1, False)))

    own_sigma = pltpu.make_async_copy(sigma_ref, sig.at[q], sig_local)
    own_sigma.start()
    own_prop = pltpu.make_async_copy(prop_hbm, prop_ref, prop_sem)
    own_prop.start()

    barrier = pltpu.get_barrier_semaphore()
    for d in range(1, f):
        tell(barrier, fin=(q + d) % f)
    for d in range(1, PLANE):
        tell(barrier, mid=mate(d))
    for p in range(1, planes):
        @pl.when(z < p)
        def _():
            tell(barrier, mid=p * PLANE + xy)

    def s_copies():
        return [
            pltpu.make_async_copy(
                sigma_ref.at[k, pl.ds(0, k)],
                sbuf.at[q, pl.ds(k * (k - 1) // 2, k)],
                s_local.at[k - 1],
            )
            for k in range(1, steps)
        ]

    @pl.when(m == 0)
    def _():
        for copy in s_copies():
            copy.start()

    loads = []
    for i, pair in enumerate(order):
        for j, c in enumerate(pair):
            copy = pltpu.make_async_copy(
                hist_ref.at[:, c], hist.at[c], hist_sem.at[2 * i + j]
            )
            loads.append(copy)
    for copy in loads[:2]:
        copy.start()

    def block_of(g, p):
        return outb.at[p, :, pl.ds(g * PLANE, PLANE)]

    zeros[...] = jnp.zeros_like(zeros)
    for g in range(groups):
        for p in range(planes):
            @pl.when(jnp.logical_not(active(p, g)))
            def _():
                pltpu.make_async_copy(zeros, block_of(g, p), o_recv.at[g, p]).start()

    def build(fq):
        lane = lax.broadcasted_iota(jnp.int32, (rf, lanes), 1)
        is_last = (m == n - 1).astype(F32)
        for k in range(steps):
            for t in range(slots // 2):
                a, b = sig[fq, k, 2 * t], sig[fq, k, 2 * t + 1]
                if 2 * t < k:
                    a = a * (m * slots + 2 * t >= k).astype(F32)
                if 2 * t + 1 < k:
                    b = b * (m * slots + 2 * t + 1 >= k).astype(F32)
                if k == 0 and 2 * t + 2 == slots:
                    b = b + prop_ref[pl.ds(pl.multiple_of(fq * rf, rf), rf)] * is_last
                real = jnp.where(lane < half, a, pltpu.roll(b, half, 1))
                imag = jnp.where(lane < half, pltpu.roll(a, half, 1), b)
                for part_id, value in enumerate((real, imag)):
                    row = (part_id * steps + k) * rf
                    high, low = split(value)
                    lhs[fq, row:row + rf, t * lanes:(t + 1) * lanes] = high
                    lhs[fq, row:row + rf, depth + t * lanes:depth + (t + 1) * lanes] = low

    own_sigma.wait()
    own_prop.wait()
    for copy in loads[2:]:
        copy.start()
    build(q)
    pl.semaphore_wait(barrier, f - 1 + PLANE - 1 + z)

    sig_out = []
    for d in range(1, f):
        copy = remote(sigma_ref, sig.at[q], sig_send.at[d], sig_recv.at[q], fin=(q + d) % f)
        copy.start()
        sig_out.append(copy)

    for d in range(1, PLANE):
        tell(greet, mid=mate(d))
    for p in range(planes - 1):
        @pl.when(z > p)
        def _():
            tell(greet, mid=p * PLANE + xy)

    pairs = sbuf.shape[1]
    cuts = (0, pairs // 2, pairs)
    chunks = range(len(cuts) - 1)

    def s_copy(to, slot, h):
        piece = sbuf.at[q, pl.ds(cuts[h], cuts[h + 1] - cuts[h])]
        return remote(piece, piece, s_send.at[slot, h], s_recv.at[h], mid=to)

    def s_first(to, h):
        return s_copy(to, to, h)

    def s_second(p, h):
        return s_copy(p * PLANE + xy, PLANE + p, h)

    firsts = (2, 3, 1)

    @pl.when(m == 0)
    def _():
        for copy in s_copies():
            copy.wait()
        for h in chunks:
            for to in firsts:
                s_first(to, h).start()

    def prepare(i):
        for j, c in enumerate(order[i]):
            loads[2 * i + j].wait()

        @pl.when(active(z, i % groups))
        def _():
            for j, c in enumerate(order[i]):
                start = col_time(c, q)
                for s in range(slots):
                    keep = (m * slots + s >= start).astype(F32)
                    high, low = split(hist[c, s] * keep)
                    rhs[i, s * half:(s + 1) * half, j * lanes:(j + 1) * lanes] = high
                    rhs[i, depth + s * half:depth + (s + 1) * half, j * lanes:(j + 1) * lanes] = low

    def compute(i, fq):
        dot = functools.partial(jnp.dot, preferred_element_type=F32)
        total = dot(lhs[fq, :, :depth], rhs[i, :depth])
        total = total + dot(lhs[fq, :, :depth], rhs[i, depth:])
        total = total + dot(lhs[fq, :, depth:], rhs[i, :depth])
        many = steps * rf
        for j, c in enumerate(order[i]):
            block = total[:, j * lanes:(j + 1) * lanes]
            part[c, fq] = block[:many] + turn(block[many:])

    def x1_copy(g, j, fq):
        return remote(
            part.at[order[g][j], fq], rx1.at[g, j, fq],
            x1_send.at[g, j, fq], x1_recv.at[g, j, fq], mid=partner1,
        )

    def x2_copy(g, fq):
        return remote(
            part.at[order[groups + g][0], fq], rx2.at[g, fq],
            x2_send.at[g, fq], x2_recv.at[g, fq], mid=partner2,
        )

    def send(g, fq):
        @pl.when(active(z, g))
        def _():
            compute(g, fq)
            for j in range(2):
                x1_copy(g, j, fq).start()

    def hold(g, fq):
        @pl.when(active(z, g))
        def _():
            compute(groups + g, fq)

    def forward(g, fq):
        @pl.when(active(z, g))
        def _():
            c = order[groups + g][0]
            x1_copy(g, 0, fq).wait_recv()
            part[c, fq] = part[c, fq] + rx1[g, 0, fq]
            x2_copy(g, fq).start()

    for g in range(groups):
        prepare(g)
        send(g, q)
    others = [(q + r) % f for r in range(1, f)]
    for r, fq in enumerate(others):
        remote(sigma_ref, sig.at[fq], sig_send.at[1 + r], sig_recv.at[fq], fin=fq).wait_recv()
        build(fq)
        for g in range(groups):
            send(g, fq)

    pl.semaphore_wait(greet, PLANE - 1 + planes - 1 - z)

    @pl.when(z == 0)
    def _():
        for h in chunks:
            @pl.when(m != 0)
            def _():
                s_first(0, h).wait_recv()
            s_second(planes - 1, h).start()
        for p in reversed(range(1, planes - 1)):
            for h in chunks:
                s_second(p, h).start()

    for g in range(groups):
        prepare(groups + g)
        for fq in (q, *others):
            hold(g, fq)
        for fq in (q, *others):
            forward(g, fq)

    @pl.when(z != 0)
    def _():
        for h in chunks:
            s_second(0, h).wait_recv()

    sx_out = []
    for d in range(1, f):
        copy = remote(sbuf.at[q], sbuf.at[q], sx_send.at[d], sx_recv.at[q], fin=(q + d) % f)
        copy.start()
        sx_out.append(copy)
    for fq in others:
        remote(sbuf.at[fq], sbuf.at[fq], sx_send.at[0], sx_recv.at[fq], fin=fq).wait_recv()

    dot = functools.partial(jnp.dot, preferred_element_type=F32)

    def exact(left, right):
        left_high, left_low = split(left)
        right_high, right_low = split(right)
        return dot(left_high, right_high) + dot(left_high, right_low) + dot(left_low, right_high)

    direct, whole = {}, {}
    for k in range(1, steps):
        for j in range(k):
            pieces = [sbuf[fq, k * (k - 1) // 2 + j] for fq in range(f)]
            block = jnp.concatenate(pieces, axis=0)
            direct[k, j] = block + prop_ref[...] if k == j + 1 else block
    for k in range(1, steps):
        for j in range(steps - 1):
            block = direct[k, j] if j < k else jnp.zeros((rows, lanes), F32)
            for i in range(j + 1, k):
                block = block + exact(direct[k, i], stack(whole[i, j]))
            whole[k, j] = block
            high, low = split(block)
            weights[0, (k - 1) * rows:k * rows, j * lanes:(j + 1) * lanes] = high
            weights[1, (k - 1) * rows:k * rows, j * lanes:(j + 1) * lanes] = low

    def o_copy(g, to):
        return remote(stage.at[g, to], outb.at[z, :, g * PLANE + xy], o_send.at[g], o_recv.at[g, z], mid=to)

    def finish(g):
        c = order[groups + g][1]
        row = []
        for fq in (q, *others):
            x1_copy(g, 1, fq).wait_recv()
            x2_copy(g, fq).wait_recv()
        for fq in range(f):
            part[c, fq] = part[c, fq] + rx1[g, 1, fq] + rx2[g, fq]
        for k in range(steps):
            pieces = [part[c, fq, k * rf:(k + 1) * rf] for fq in range(f)]
            row.append(jnp.concatenate(pieces, axis=0))
        high, low = split(jnp.concatenate([stack(row[k]) for k in range(steps - 1)], axis=0))
        dot = functools.partial(jnp.dot, preferred_element_type=F32)
        terms = dot(weights[0], high) + dot(weights[0], low) + dot(weights[1], high)
        for k in range(steps):
            value = row[k]
            if k > 0:
                value = value + terms[(k - 1) * rows:k * rows]
            for to in range(n):
                stage[g, to, k] = value[to * rc:(to + 1) * rc]
        for p in range(planes):
            for d in range(PLANE):
                to = p * PLANE + (xy + d) % PLANE
                if d:
                    o_copy(g, to).start()
                else:
                    @pl.when(p != z)
                    def _():
                        o_copy(g, to).start()
        pltpu.make_async_copy(stage.at[g, m], outb.at[z, :, g * PLANE + xy], o_recv.at[g, z]).start()

    for g in range(groups):
        @pl.when(active(z, g))
        def _():
            finish(g)

    for g in range(groups):
        for p in range(planes):
            pltpu.make_async_copy(block_of(g, p), block_of(g, p), o_recv.at[g, p]).wait()

    for copy in sig_out + sx_out:
        copy.wait_send()

    @pl.when(m == 0)
    def _():
        for h in chunks:
            for to in firsts:
                s_first(to, h).wait_send()

    @pl.when(z == 0)
    def _():
        for p in range(1, planes):
            for h in chunks:
                s_second(p, h).wait_send()

    for g in range(groups):
        @pl.when(active(z, g))
        def _():
            for fq in range(f):
                x1_copy(g, 0, fq).wait_send()
                x1_copy(g, 1, fq).wait_send()
                x2_copy(g, fq).wait_send()
            sent = stage.at[g, pl.ds(0, n - 1)]
            pltpu.make_async_copy(sent, sent, o_send.at[g]).wait()


def solution(mesh):
    n, f = mesh.shape["mid"], mesh.shape["fin"]

    def on_device(history, sigma, propagator):
        slots, cols, rows, lanes = history.shape
        steps, rf = sigma.shape[0], sigma.shape[2]
        rc, depth = rows // n, slots * lanes // 2
        planes, groups, pairs = n // PLANE, cols // PLANE, steps * (steps - 1) // 2
        many = steps * rf
        dma = pltpu.SemaphoreType.DMA
        anywhere = pl.BlockSpec(memory_space=pl.ANY)
        out = pl.pallas_call(
            functools.partial(kernel, n, f),
            out_shape=jax.ShapeDtypeStruct((planes, steps, cols, rc, lanes), F32),
            in_specs=[anywhere, anywhere, anywhere],
            out_specs=anywhere,
            scratch_shapes=[
                pltpu.VMEM((cols, slots, rows, lanes), F32),
                pltpu.VMEM((f, steps, slots, rf, lanes), F32),
                pltpu.VMEM((rows, lanes), F32),
                pltpu.VMEM((f, pairs, rf, lanes), F32),
                pltpu.VMEM((f, 2 * many, 2 * depth), BF16),
                pltpu.VMEM((2 * groups, 2 * depth, 2 * lanes), BF16),
                pltpu.VMEM((cols, f, many, lanes), F32),
                pltpu.VMEM((groups, 2, f, many, lanes), F32),
                pltpu.VMEM((groups, f, many, lanes), F32),
                pltpu.VMEM((2, (steps - 1) * rows, (steps - 1) * lanes), BF16),
                pltpu.VMEM((groups, n, steps, rc, lanes), F32),
                pltpu.VMEM((steps, PLANE, rc, lanes), F32),
                dma((cols,)), dma, dma, dma((f,)), dma((f,)),
                dma((steps - 1,)), dma((PLANE + planes, 2)), dma((2,)),
                dma((f,)), dma((f,)), pltpu.SemaphoreType.REGULAR,
                dma((groups, 2, f)), dma((groups, 2, f)), dma((groups, f)), dma((groups, f)),
                dma((groups,)), dma((groups, planes)),
            ],
            compiler_params=pltpu.CompilerParams(
                collective_id=0, has_side_effects=True, vmem_limit_bytes=40 * 2**20
            ),
        )(*(pltpu.with_memory_space_constraint(a, pltpu.HBM) for a in (history, sigma, propagator)))
        return jnp.sum(out, axis=0)

    in_specs = (P("mid", "fin", None, None), P(None, "mid", "fin", None), P())
    return jax.shard_map(
        on_device, mesh=mesh, in_specs=in_specs, out_specs=P(None, "fin", "mid", None),
        check_vma=False,
    )
```

```python
import functools

import jax
import jax.numpy as jnp
from jax import lax
from jax.experimental import pallas as pl
from jax.experimental.pallas import tpu as pltpu
from jax.sharding import PartitionSpec as P

MESH = pl.DeviceIdType.MESH
PLANE = 4
F32 = jnp.float32
BF16 = jnp.bfloat16


def split(value):
    high = value.astype(BF16)
    return high, (value - high.astype(F32)).astype(BF16)


def turn(value):
    half = value.shape[-1] // 2
    rolled = pltpu.roll(value, half, 1)
    lane = lax.broadcasted_iota(jnp.int32, value.shape, 1)
    return jnp.where(lane < half, -rolled, rolled)


def stack(value):
    return jnp.concatenate([value, turn(value)], axis=0)


def kernel(
    n, f, hist_ref, sigma_ref, prop_hbm, outb,
    hist, sig, prop_ref, sbuf, lhs, rhs, part, rx1, rx2, weights, stage, zeros,
    hist_sem, prop_sem, sig_local, sig_send, sig_recv, s_local, s_send, s_recv,
    sx_send, sx_recv, greet, x1_send, x1_recv, x2_send, x2_recv, o_send, o_recv,
):
    m = lax.axis_index("mid")
    q = lax.axis_index("fin")
    slots, cols, rows, lanes = hist_ref.shape
    steps, rf = sigma_ref.shape[0], sigma_ref.shape[2]
    width, ncol = n * slots, f * cols
    planes, groups = n // PLANE, cols // PLANE
    rc = rows // n
    half = lanes // 2
    depth = slots * half
    x, y, z = m % 2, (m // 2) % 2, m // PLANE
    xy = m % PLANE
    base = m - xy
    o = (q + (z == 0).astype(jnp.int32)) % 2
    b1, b2 = x + o * (y - x), y + o * (x - y)
    w1, w2 = 1 + o, 2 - o
    partner1, partner2 = m + w1 * (1 - 2 * b1), m + w2 * (1 - 2 * b2)

    def remote(src, dst, send, recv, **where):
        return pltpu.make_async_remote_copy(
            src_ref=src, dst_ref=dst, send_sem=send, recv_sem=recv,
            device_id=where, device_id_type=MESH,
        )

    def tell(sem, **where):
        pl.semaphore_signal(sem, inc=1, device_id=where, device_id_type=MESH)

    def mate(d):
        return base + (xy + d) % PLANE

    def col_time(local, fin):
        return ((fin * cols + local) * width) // ncol

    def active(plane, g):
        return (plane * PLANE + PLANE) * slots - 1 >= col_time(g * PLANE, q)

    def column(g, flip1, flip2):
        c1 = 1 - b1 if flip1 else b1
        c2 = 1 - b2 if flip2 else b2
        return g * PLANE + c1 * w1 + c2 * w2

    order = []
    for flip1 in (True, False):
        for g in range(groups):
            order.append((column(g, flip1, True), column(g, flip1, False)))

    own_sigma = pltpu.make_async_copy(sigma_ref, sig.at[q], sig_local)
    own_sigma.start()
    own_prop = pltpu.make_async_copy(prop_hbm, prop_ref, prop_sem)
    own_prop.start()

    barrier = pltpu.get_barrier_semaphore()
    for d in range(1, f):
        tell(barrier, fin=(q + d) % f)
    for d in range(1, PLANE):
        tell(barrier, mid=mate(d))
    for p in range(1, planes):
        @pl.when(z < p)
        def _():
            tell(barrier, mid=p * PLANE + xy)

    def s_copies():
        return [
            pltpu.make_async_copy(
                sigma_ref.at[k, pl.ds(0, k)],
                sbuf.at[q, pl.ds(k * (k - 1) // 2, k)],
                s_local.at[k - 1],
            )
            for k in range(1, steps)
        ]

    @pl.when(m == 0)
    def _():
        for copy in s_copies():
            copy.start()

    loads = []
    for i, pair in enumerate(order):
        for j, c in enumerate(pair):
            copy = pltpu.make_async_copy(
                hist_ref.at[:, c], hist.at[c], hist_sem.at[2 * i + j]
            )
            loads.append(copy)
    for copy in loads[:2]:
        copy.start()

    def block_of(g, p):
        return outb.at[p, :, pl.ds(g * PLANE, PLANE)]

    zeros[...] = jnp.zeros_like(zeros)
    for g in range(groups):
        for p in range(planes):
            @pl.when(jnp.logical_not(active(p, g)))
            def _():
                pltpu.make_async_copy(zeros, block_of(g, p), o_recv.at[g, p]).start()

    def build(fq):
        lane = lax.broadcasted_iota(jnp.int32, (rf, lanes), 1)
        is_last = (m == n - 1).astype(F32)
        for k in range(steps):
            for t in range(slots // 2):
                a, b = sig[fq, k, 2 * t], sig[fq, k, 2 * t + 1]
                if 2 * t < k:
                    a = a * (m * slots + 2 * t >= k).astype(F32)
                if 2 * t + 1 < k:
                    b = b * (m * slots + 2 * t + 1 >= k).astype(F32)
                if k == 0 and 2 * t + 2 == slots:
                    b = b + prop_ref[pl.ds(pl.multiple_of(fq * rf, rf), rf)] * is_last
                real = jnp.where(lane < half, a, pltpu.roll(b, half, 1))
                imag = jnp.where(lane < half, pltpu.roll(a, half, 1), b)
                for part_id, value in enumerate((real, imag)):
                    row = (part_id * steps + k) * rf
                    high, low = split(value)
                    lhs[fq, row:row + rf, t * lanes:(t + 1) * lanes] = high
                    lhs[fq, row:row + rf, depth + t * lanes:depth + (t + 1) * lanes] = low

    own_sigma.wait()
    own_prop.wait()
    for copy in loads[2:]:
        copy.start()
    build(q)
    pl.semaphore_wait(barrier, f - 1 + PLANE - 1 + z)

    sig_out = []
    for d in range(1, f):
        copy = remote(sigma_ref, sig.at[q], sig_send.at[d], sig_recv.at[q], fin=(q + d) % f)
        copy.start()
        sig_out.append(copy)

    for d in range(1, PLANE):
        tell(greet, mid=mate(d))
    for p in range(planes - 1):
        @pl.when(z > p)
        def _():
            tell(greet, mid=p * PLANE + xy)

    pairs = sbuf.shape[1]
    chunks = range(pairs)

    def s_copy(to, slot, h):
        piece = sbuf.at[q, h]
        return remote(piece, piece, s_send.at[slot, h], s_recv.at[h], mid=to)

    def s_first(to, h):
        return s_copy(to, to, h)

    def s_second(p, h):
        return s_copy(p * PLANE + xy, PLANE + p, h)

    firsts = (2, 3, 1)

    @pl.when(m == 0)
    def _():
        for copy in s_copies():
            copy.wait()
        for h in chunks:
            for to in firsts:
                s_first(to, h).start()

    def prepare(i):
        for j, c in enumerate(order[i]):
            loads[2 * i + j].wait()

        @pl.when(active(z, i % groups))
        def _():
            for j, c in enumerate(order[i]):
                start = col_time(c, q)
                for s in range(slots):
                    keep = (m * slots + s >= start).astype(F32)
                    high, low = split(hist[c, s] * keep)
                    rhs[i, s * half:(s + 1) * half, j * lanes:(j + 1) * lanes] = high
                    rhs[i, depth + s * half:depth + (s + 1) * half, j * lanes:(j + 1) * lanes] = low

    def compute(i, fq):
        dot = functools.partial(jnp.dot, preferred_element_type=F32)
        total = dot(lhs[fq, :, :depth], rhs[i, :depth])
        total = total + dot(lhs[fq, :, :depth], rhs[i, depth:])
        total = total + dot(lhs[fq, :, depth:], rhs[i, :depth])
        many = steps * rf
        for j, c in enumerate(order[i]):
            block = total[:, j * lanes:(j + 1) * lanes]
            part[c, fq] = block[:many] + turn(block[many:])

    def x1_copy(g, j, fq):
        return remote(
            part.at[order[g][j], fq], rx1.at[g, j, fq],
            x1_send.at[g, j, fq], x1_recv.at[g, j, fq], mid=partner1,
        )

    def x2_copy(g, fq):
        return remote(
            part.at[order[groups + g][0], fq], rx2.at[g, fq],
            x2_send.at[g, fq], x2_recv.at[g, fq], mid=partner2,
        )

    def send(g, fq):
        @pl.when(active(z, g))
        def _():
            compute(g, fq)
            for j in range(2):
                x1_copy(g, j, fq).start()

    def hold(g, fq):
        @pl.when(active(z, g))
        def _():
            compute(groups + g, fq)

    def forward(g, fq):
        @pl.when(active(z, g))
        def _():
            c = order[groups + g][0]
            x1_copy(g, 0, fq).wait_recv()
            part[c, fq] = part[c, fq] + rx1[g, 0, fq]
            x2_copy(g, fq).start()

    for g in range(groups):
        prepare(g)
        send(g, q)
    others = [(q + r) % f for r in range(1, f)]
    for r, fq in enumerate(others):
        remote(sigma_ref, sig.at[fq], sig_send.at[1 + r], sig_recv.at[fq], fin=fq).wait_recv()
        build(fq)
        for g in range(groups):
            send(g, fq)

    pl.semaphore_wait(greet, PLANE - 1 + planes - 1 - z)

    @pl.when(z == 0)
    def _():
        for h in chunks:
            @pl.when(m != 0)
            def _():
                s_first(0, h).wait_recv()
            for p in reversed(range(planes // 2, planes)):
                s_second(p, h).start()
        for p in reversed(range(1, planes // 2)):
            for h in chunks:
                s_second(p, h).start()

    for g in range(groups):
        prepare(groups + g)
        for fq in (q, *others):
            hold(g, fq)
        for fq in (q, *others):
            forward(g, fq)

    @pl.when(z != 0)
    def _():
        for h in chunks:
            s_second(0, h).wait_recv()

    sx_out = []
    for d in range(1, f):
        copy = remote(sbuf.at[q], sbuf.at[q], sx_send.at[d], sx_recv.at[q], fin=(q + d) % f)
        copy.start()
        sx_out.append(copy)
    for fq in others:
        remote(sbuf.at[fq], sbuf.at[fq], sx_send.at[0], sx_recv.at[fq], fin=fq).wait_recv()

    dot = functools.partial(jnp.dot, preferred_element_type=F32)

    def exact(left, right):
        left_high, left_low = split(left)
        right_high, right_low = split(right)
        return dot(left_high, right_high) + dot(left_high, right_low) + dot(left_low, right_high)

    direct, whole = {}, {}
    for k in range(1, steps):
        for j in range(k):
            pieces = [sbuf[fq, k * (k - 1) // 2 + j] for fq in range(f)]
            block = jnp.concatenate(pieces, axis=0)
            direct[k, j] = block + prop_ref[...] if k == j + 1 else block
    for k in range(1, steps):
        for j in range(steps - 1):
            block = direct[k, j] if j < k else jnp.zeros((rows, lanes), F32)
            for i in range(j + 1, k):
                block = block + exact(direct[k, i], stack(whole[i, j]))
            whole[k, j] = block
            high, low = split(block)
            weights[0, (k - 1) * rows:k * rows, j * lanes:(j + 1) * lanes] = high
            weights[1, (k - 1) * rows:k * rows, j * lanes:(j + 1) * lanes] = low

    def o_copy(g, to):
        return remote(stage.at[g, to], outb.at[z, :, g * PLANE + xy], o_send.at[g], o_recv.at[g, z], mid=to)

    def finish(g):
        c = order[groups + g][1]
        row = []
        for fq in (q, *others):
            x1_copy(g, 1, fq).wait_recv()
            x2_copy(g, fq).wait_recv()
        for fq in range(f):
            part[c, fq] = part[c, fq] + rx1[g, 1, fq] + rx2[g, fq]
        for k in range(steps):
            pieces = [part[c, fq, k * rf:(k + 1) * rf] for fq in range(f)]
            row.append(jnp.concatenate(pieces, axis=0))
        high, low = split(jnp.concatenate([stack(row[k]) for k in range(steps - 1)], axis=0))
        dot = functools.partial(jnp.dot, preferred_element_type=F32)
        terms = dot(weights[0], high) + dot(weights[0], low) + dot(weights[1], high)
        for k in range(steps):
            value = row[k]
            if k > 0:
                value = value + terms[(k - 1) * rows:k * rows]
            for to in range(n):
                stage[g, to, k] = value[to * rc:(to + 1) * rc]
        for p in range(planes):
            for d in range(PLANE):
                to = p * PLANE + (xy + d) % PLANE
                if d:
                    o_copy(g, to).start()
                else:
                    @pl.when(p != z)
                    def _():
                        o_copy(g, to).start()
        pltpu.make_async_copy(stage.at[g, m], outb.at[z, :, g * PLANE + xy], o_recv.at[g, z]).start()

    for g in range(groups):
        @pl.when(active(z, g))
        def _():
            finish(g)

    for g in range(groups):
        for p in range(planes):
            pltpu.make_async_copy(block_of(g, p), block_of(g, p), o_recv.at[g, p]).wait()

    for copy in sig_out + sx_out:
        copy.wait_send()

    @pl.when(m == 0)
    def _():
        for h in chunks:
            for to in firsts:
                s_first(to, h).wait_send()

    @pl.when(z == 0)
    def _():
        for p in range(1, planes):
            for h in chunks:
                s_second(p, h).wait_send()

    for g in range(groups):
        @pl.when(active(z, g))
        def _():
            for fq in range(f):
                x1_copy(g, 0, fq).wait_send()
                x1_copy(g, 1, fq).wait_send()
                x2_copy(g, fq).wait_send()
            sent = stage.at[g, pl.ds(0, n - 1)]
            pltpu.make_async_copy(sent, sent, o_send.at[g]).wait()


def solution(mesh):
    n, f = mesh.shape["mid"], mesh.shape["fin"]

    def on_device(history, sigma, propagator):
        slots, cols, rows, lanes = history.shape
        steps, rf = sigma.shape[0], sigma.shape[2]
        rc, depth = rows // n, slots * lanes // 2
        planes, groups, pairs = n // PLANE, cols // PLANE, steps * (steps - 1) // 2
        many = steps * rf
        dma = pltpu.SemaphoreType.DMA
        anywhere = pl.BlockSpec(memory_space=pl.ANY)
        out = pl.pallas_call(
            functools.partial(kernel, n, f),
            out_shape=jax.ShapeDtypeStruct((planes, steps, cols, rc, lanes), F32),
            in_specs=[anywhere, anywhere, anywhere],
            out_specs=anywhere,
            scratch_shapes=[
                pltpu.VMEM((cols, slots, rows, lanes), F32),
                pltpu.VMEM((f, steps, slots, rf, lanes), F32),
                pltpu.VMEM((rows, lanes), F32),
                pltpu.VMEM((f, pairs, rf, lanes), F32),
                pltpu.VMEM((f, 2 * many, 2 * depth), BF16),
                pltpu.VMEM((2 * groups, 2 * depth, 2 * lanes), BF16),
                pltpu.VMEM((cols, f, many, lanes), F32),
                pltpu.VMEM((groups, 2, f, many, lanes), F32),
                pltpu.VMEM((groups, f, many, lanes), F32),
                pltpu.VMEM((2, (steps - 1) * rows, (steps - 1) * lanes), BF16),
                pltpu.VMEM((groups, n, steps, rc, lanes), F32),
                pltpu.VMEM((steps, PLANE, rc, lanes), F32),
                dma((cols,)), dma, dma, dma((f,)), dma((f,)),
                dma((steps - 1,)), dma((PLANE + planes, pairs)), dma((pairs,)),
                dma((f,)), dma((f,)), pltpu.SemaphoreType.REGULAR,
                dma((groups, 2, f)), dma((groups, 2, f)), dma((groups, f)), dma((groups, f)),
                dma((groups,)), dma((groups, planes)),
            ],
            compiler_params=pltpu.CompilerParams(
                collective_id=0, has_side_effects=True, vmem_limit_bytes=40 * 2**20
            ),
        )(*(pltpu.with_memory_space_constraint(a, pltpu.HBM) for a in (history, sigma, propagator)))
        return jnp.sum(out, axis=0)

    in_specs = (P("mid", "fin", None, None), P(None, "mid", "fin", None), P())
    return jax.shard_map(
        on_device, mesh=mesh, in_specs=in_specs, out_specs=P(None, "fin", "mid", None),
        check_vma=False,
    )
```

```python
import functools

import jax
import jax.numpy as jnp
from jax import lax
from jax.experimental import pallas as pl
from jax.experimental.pallas import tpu as pltpu
from jax.sharding import PartitionSpec as P

MESH = pl.DeviceIdType.MESH
PLANE = 4
F32 = jnp.float32
BF16 = jnp.bfloat16


def split(value):
    high = value.astype(BF16)
    return high, (value - high.astype(F32)).astype(BF16)


def turn(value):
    half = value.shape[-1] // 2
    rolled = pltpu.roll(value, half, 1)
    lane = lax.broadcasted_iota(jnp.int32, value.shape, 1)
    return jnp.where(lane < half, -rolled, rolled)


def stack(value):
    return jnp.concatenate([value, turn(value)], axis=0)


def kernel(
    n, f, hist_ref, sigma_ref, prop_hbm, outb,
    hist, sig, prop_ref, sbuf, lhs, rhs, part, rx1, rx2, weights, stage, zeros,
    hist_sem, prop_sem, sig_local, sig_send, sig_recv, s_local, s_send, s_recv,
    sx_send, sx_recv, greet, x1_send, x1_recv, x2_send, x2_recv, o_send, o_recv,
):
    m = lax.axis_index("mid")
    q = lax.axis_index("fin")
    slots, cols, rows, lanes = hist_ref.shape
    steps, rf = sigma_ref.shape[0], sigma_ref.shape[2]
    width, ncol = n * slots, f * cols
    planes, groups = n // PLANE, cols // PLANE
    rc = rows // n
    half = lanes // 2
    depth = slots * half
    x, y, z = m % 2, (m // 2) % 2, m // PLANE
    xy = m % PLANE
    base = m - xy
    o = (q + (z == 0).astype(jnp.int32)) % 2
    b1, b2 = x + o * (y - x), y + o * (x - y)
    w1, w2 = 1 + o, 2 - o
    partner1, partner2 = m + w1 * (1 - 2 * b1), m + w2 * (1 - 2 * b2)

    def remote(src, dst, send, recv, **where):
        return pltpu.make_async_remote_copy(
            src_ref=src, dst_ref=dst, send_sem=send, recv_sem=recv,
            device_id=where, device_id_type=MESH,
        )

    def tell(sem, **where):
        pl.semaphore_signal(sem, inc=1, device_id=where, device_id_type=MESH)

    def mate(d):
        return base + (xy + d) % PLANE

    def col_time(local, fin):
        return ((fin * cols + local) * width) // ncol

    def active(plane, g):
        return (plane * PLANE + PLANE) * slots - 1 >= col_time(g * PLANE, q)

    def column(g, flip1, flip2):
        c1 = 1 - b1 if flip1 else b1
        c2 = 1 - b2 if flip2 else b2
        return g * PLANE + c1 * w1 + c2 * w2

    order = []
    for flip1 in (True, False):
        for g in range(groups):
            order.append((column(g, flip1, True), column(g, flip1, False)))

    own_sigma = pltpu.make_async_copy(sigma_ref, sig.at[q], sig_local)
    own_sigma.start()
    own_prop = pltpu.make_async_copy(prop_hbm, prop_ref, prop_sem)
    own_prop.start()

    barrier = pltpu.get_barrier_semaphore()
    for d in range(1, f):
        tell(barrier, fin=(q + d) % f)
    for d in range(1, PLANE):
        tell(barrier, mid=mate(d))
    for p in range(1, planes):
        @pl.when(z < p)
        def _():
            tell(barrier, mid=p * PLANE + xy)

    def s_copies():
        return [
            pltpu.make_async_copy(
                sigma_ref.at[k, pl.ds(0, k)],
                sbuf.at[q, pl.ds(k * (k - 1) // 2, k)],
                s_local.at[k - 1],
            )
            for k in range(1, steps)
        ]

    @pl.when(m == 0)
    def _():
        for copy in s_copies():
            copy.start()

    loads = []
    for i, pair in enumerate(order):
        for j, c in enumerate(pair):
            copy = pltpu.make_async_copy(
                hist_ref.at[:, c], hist.at[c], hist_sem.at[2 * i + j]
            )
            loads.append(copy)
    for copy in loads[:2]:
        copy.start()

    def block_of(g, p):
        return outb.at[p, :, pl.ds(g * PLANE, PLANE)]

    zeros[...] = jnp.zeros_like(zeros)
    for g in range(groups):
        for p in range(planes):
            @pl.when(jnp.logical_not(active(p, g)))
            def _():
                pltpu.make_async_copy(zeros, block_of(g, p), o_recv.at[g, p]).start()

    def build(fq):
        lane = lax.broadcasted_iota(jnp.int32, (rf, lanes), 1)
        is_last = (m == n - 1).astype(F32)
        for k in range(steps):
            for t in range(slots // 2):
                a, b = sig[fq, k, 2 * t], sig[fq, k, 2 * t + 1]
                if 2 * t < k:
                    a = a * (m * slots + 2 * t >= k).astype(F32)
                if 2 * t + 1 < k:
                    b = b * (m * slots + 2 * t + 1 >= k).astype(F32)
                if k == 0 and 2 * t + 2 == slots:
                    b = b + prop_ref[pl.ds(pl.multiple_of(fq * rf, rf), rf)] * is_last
                real = jnp.where(lane < half, a, pltpu.roll(b, half, 1))
                imag = jnp.where(lane < half, pltpu.roll(a, half, 1), b)
                for part_id, value in enumerate((real, imag)):
                    row = (part_id * steps + k) * rf
                    high, low = split(value)
                    lhs[fq, row:row + rf, t * lanes:(t + 1) * lanes] = high
                    lhs[fq, row:row + rf, depth + t * lanes:depth + (t + 1) * lanes] = low

    own_sigma.wait()
    own_prop.wait()
    for copy in loads[2:]:
        copy.start()
    build(q)
    pl.semaphore_wait(barrier, f - 1 + PLANE - 1 + z)

    sig_out = []
    for d in range(1, f):
        copy = remote(sigma_ref, sig.at[q], sig_send.at[d], sig_recv.at[q], fin=(q + d) % f)
        copy.start()
        sig_out.append(copy)

    for d in range(1, PLANE):
        tell(greet, mid=mate(d))
    for p in range(planes - 1):
        @pl.when(z > p)
        def _():
            tell(greet, mid=p * PLANE + xy)

    pairs = sbuf.shape[1]
    chunks = range(pairs)

    def s_copy(to, slot, h):
        piece = sbuf.at[q, h]
        return remote(piece, piece, s_send.at[slot, h], s_recv.at[h], mid=to)

    def s_first(to, h):
        return s_copy(to, to, h)

    def s_second(p, h):
        return s_copy(p * PLANE + xy, PLANE + p, h)

    firsts = (2, 3, 1)

    @pl.when(m == 0)
    def _():
        for copy in s_copies():
            copy.wait()
        for h in chunks:
            for to in firsts:
                s_first(to, h).start()

    def prepare(i):
        for j, c in enumerate(order[i]):
            loads[2 * i + j].wait()

        @pl.when(active(z, i % groups))
        def _():
            for j, c in enumerate(order[i]):
                start = col_time(c, q)
                for s in range(slots):
                    keep = (m * slots + s >= start).astype(F32)
                    high, low = split(hist[c, s] * keep)
                    rhs[i, s * half:(s + 1) * half, j * lanes:(j + 1) * lanes] = high
                    rhs[i, depth + s * half:depth + (s + 1) * half, j * lanes:(j + 1) * lanes] = low

    def compute(i, fq):
        dot = functools.partial(jnp.dot, preferred_element_type=F32)
        total = dot(lhs[fq, :, :depth], rhs[i, :depth])
        total = total + dot(lhs[fq, :, :depth], rhs[i, depth:])
        total = total + dot(lhs[fq, :, depth:], rhs[i, :depth])
        many = steps * rf
        for j, c in enumerate(order[i]):
            block = total[:, j * lanes:(j + 1) * lanes]
            part[c, fq] = block[:many] + turn(block[many:])

    def x1_copy(g, j, fq):
        return remote(
            part.at[order[g][j], fq], rx1.at[g, j, fq],
            x1_send.at[g, j, fq], x1_recv.at[g, j, fq], mid=partner1,
        )

    def x2_copy(g, fq):
        return remote(
            part.at[order[groups + g][0], fq], rx2.at[g, fq],
            x2_send.at[g, fq], x2_recv.at[g, fq], mid=partner2,
        )

    def send(g, fq):
        @pl.when(active(z, g))
        def _():
            compute(g, fq)
            for j in range(2):
                x1_copy(g, j, fq).start()

    def hold(g, fq):
        @pl.when(active(z, g))
        def _():
            compute(groups + g, fq)

    def forward(g, fq):
        @pl.when(active(z, g))
        def _():
            c = order[groups + g][0]
            x1_copy(g, 0, fq).wait_recv()
            part[c, fq] = part[c, fq] + rx1[g, 0, fq]
            x2_copy(g, fq).start()

    for g in range(groups):
        prepare(g)
        send(g, q)
    others = [(q + r) % f for r in range(1, f)]
    for r, fq in enumerate(others):
        remote(sigma_ref, sig.at[fq], sig_send.at[1 + r], sig_recv.at[fq], fin=fq).wait_recv()
        build(fq)
        for g in range(groups):
            send(g, fq)

    pl.semaphore_wait(greet, PLANE - 1 + planes - 1 - z)

    @pl.when(z == 0)
    def _():
        for h in chunks:
            @pl.when(m != 0)
            def _():
                s_first(0, h).wait_recv()
            for p in reversed(range(planes // 2, planes)):
                s_second(p, h).start()
        for p in reversed(range(1, planes // 2)):
            for h in chunks:
                s_second(p, h).start()

    for g in range(groups):
        prepare(groups + g)
        for fq in (q, *others):
            hold(g, fq)
        for fq in (q, *others):
            forward(g, fq)

    @pl.when(z != 0)
    def _():
        for h in chunks:
            s_second(0, h).wait_recv()

    sx_out = []
    for d in range(1, f):
        copy = remote(sbuf.at[q], sbuf.at[q], sx_send.at[d], sx_recv.at[q], fin=(q + d) % f)
        copy.start()
        sx_out.append(copy)
    for fq in others:
        remote(sbuf.at[fq], sbuf.at[fq], sx_send.at[0], sx_recv.at[fq], fin=fq).wait_recv()

    dot = functools.partial(jnp.dot, preferred_element_type=F32)

    def exact(left, right):
        left_high, left_low = split(left)
        right_high, right_low = split(right)
        return dot(left_high, right_high) + dot(left_high, right_low) + dot(left_low, right_high)

    direct, whole = {}, {}
    for k in range(1, steps):
        for j in range(k):
            pieces = [sbuf[fq, k * (k - 1) // 2 + j] for fq in range(f)]
            block = jnp.concatenate(pieces, axis=0)
            direct[k, j] = block + prop_ref[...] if k == j + 1 else block
    for k in range(1, steps):
        for j in range(steps - 1):
            block = direct[k, j] if j < k else jnp.zeros((rows, lanes), F32)
            for i in range(j + 1, k):
                block = block + exact(direct[k, i], stack(whole[i, j]))
            whole[k, j] = block
            high, low = split(block)
            weights[0, (k - 1) * rows:k * rows, j * lanes:(j + 1) * lanes] = high
            weights[1, (k - 1) * rows:k * rows, j * lanes:(j + 1) * lanes] = low

    def o_copy(g, to):
        return remote(stage.at[g, to], outb.at[z, :, g * PLANE + xy], o_send.at[g], o_recv.at[g, z], mid=to)

    def finish(g):
        c = order[groups + g][1]
        row = []
        for fq in (q, *others):
            x1_copy(g, 1, fq).wait_recv()
            x2_copy(g, fq).wait_recv()
        for fq in range(f):
            part[c, fq] = part[c, fq] + rx1[g, 1, fq] + rx2[g, fq]
        for k in range(steps):
            pieces = [part[c, fq, k * rf:(k + 1) * rf] for fq in range(f)]
            row.append(jnp.concatenate(pieces, axis=0))
        high, low = split(jnp.concatenate([stack(row[k]) for k in range(steps - 1)], axis=0))
        dot = functools.partial(jnp.dot, preferred_element_type=F32)
        terms = dot(weights[0], high) + dot(weights[0], low) + dot(weights[1], high)
        for k in range(steps):
            value = row[k]
            if k > 0:
                value = value + terms[(k - 1) * rows:k * rows]
            for to in range(n):
                stage[g, to, k] = value[to * rc:(to + 1) * rc]
        for to in range(n):
            @pl.when(to != m)
            def _():
                o_copy(g, to).start()
        pltpu.make_async_copy(stage.at[g, m], outb.at[z, :, g * PLANE + xy], o_recv.at[g, z]).start()

    for g in range(groups):
        @pl.when(active(z, g))
        def _():
            finish(g)

    for g in range(groups):
        for p in range(planes):
            pltpu.make_async_copy(block_of(g, p), block_of(g, p), o_recv.at[g, p]).wait()

    for copy in sig_out + sx_out:
        copy.wait_send()

    @pl.when(m == 0)
    def _():
        for h in chunks:
            for to in firsts:
                s_first(to, h).wait_send()

    @pl.when(z == 0)
    def _():
        for p in range(1, planes):
            for h in chunks:
                s_second(p, h).wait_send()

    for g in range(groups):
        @pl.when(active(z, g))
        def _():
            for fq in range(f):
                x1_copy(g, 0, fq).wait_send()
                x1_copy(g, 1, fq).wait_send()
                x2_copy(g, fq).wait_send()
            sent = stage.at[g, pl.ds(0, n - 1)]
            pltpu.make_async_copy(sent, sent, o_send.at[g]).wait()


def solution(mesh):
    n, f = mesh.shape["mid"], mesh.shape["fin"]

    def on_device(history, sigma, propagator):
        slots, cols, rows, lanes = history.shape
        steps, rf = sigma.shape[0], sigma.shape[2]
        rc, depth = rows // n, slots * lanes // 2
        planes, groups, pairs = n // PLANE, cols // PLANE, steps * (steps - 1) // 2
        many = steps * rf
        dma = pltpu.SemaphoreType.DMA
        anywhere = pl.BlockSpec(memory_space=pl.ANY)
        out = pl.pallas_call(
            functools.partial(kernel, n, f),
            out_shape=jax.ShapeDtypeStruct((planes, steps, cols, rc, lanes), F32),
            in_specs=[anywhere, anywhere, anywhere],
            out_specs=anywhere,
            scratch_shapes=[
                pltpu.VMEM((cols, slots, rows, lanes), F32),
                pltpu.VMEM((f, steps, slots, rf, lanes), F32),
                pltpu.VMEM((rows, lanes), F32),
                pltpu.VMEM((f, pairs, rf, lanes), F32),
                pltpu.VMEM((f, 2 * many, 2 * depth), BF16),
                pltpu.VMEM((2 * groups, 2 * depth, 2 * lanes), BF16),
                pltpu.VMEM((cols, f, many, lanes), F32),
                pltpu.VMEM((groups, 2, f, many, lanes), F32),
                pltpu.VMEM((groups, f, many, lanes), F32),
                pltpu.VMEM((2, (steps - 1) * rows, (steps - 1) * lanes), BF16),
                pltpu.VMEM((groups, n, steps, rc, lanes), F32),
                pltpu.VMEM((steps, PLANE, rc, lanes), F32),
                dma((cols,)), dma, dma, dma((f,)), dma((f,)),
                dma((steps - 1,)), dma((PLANE + planes, pairs)), dma((pairs,)),
                dma((f,)), dma((f,)), pltpu.SemaphoreType.REGULAR,
                dma((groups, 2, f)), dma((groups, 2, f)), dma((groups, f)), dma((groups, f)),
                dma((groups,)), dma((groups, planes)),
            ],
            compiler_params=pltpu.CompilerParams(
                collective_id=0, has_side_effects=True, vmem_limit_bytes=40 * 2**20
            ),
        )(*(pltpu.with_memory_space_constraint(a, pltpu.HBM) for a in (history, sigma, propagator)))
        return jnp.sum(out, axis=0)

    in_specs = (P("mid", "fin", None, None), P(None, "mid", "fin", None), P())
    return jax.shard_map(
        on_device, mesh=mesh, in_specs=in_specs, out_specs=P(None, "fin", "mid", None),
        check_vma=False,
    )
```

```python
import functools

import jax
import jax.numpy as jnp
from jax import lax
from jax.experimental import pallas as pl
from jax.experimental.pallas import tpu as pltpu
from jax.sharding import PartitionSpec as P

MESH = pl.DeviceIdType.MESH
PLANE = 4
F32 = jnp.float32
BF16 = jnp.bfloat16


def split(value):
    high = value.astype(BF16)
    return high, (value - high.astype(F32)).astype(BF16)


def turn(value):
    half = value.shape[-1] // 2
    rolled = pltpu.roll(value, half, 1)
    lane = lax.broadcasted_iota(jnp.int32, value.shape, 1)
    return jnp.where(lane < half, -rolled, rolled)


def stack(value):
    return jnp.concatenate([value, turn(value)], axis=0)


def kernel(
    n, f, hist_ref, sigma_ref, prop_hbm, outb,
    hist, sig, prop_ref, sbuf, lhs, rhs, part, rx1, rx2, weights, stage, zeros,
    hist_sem, prop_sem, sig_local, sig_send, sig_recv, s_local, s_send, s_recv,
    sx_send, sx_recv, greet, x1_send, x1_recv, x2_send, x2_recv, o_send, o_recv,
):
    m = lax.axis_index("mid")
    q = lax.axis_index("fin")
    slots, cols, rows, lanes = hist_ref.shape
    steps, rf = sigma_ref.shape[0], sigma_ref.shape[2]
    width, ncol = n * slots, f * cols
    planes, groups = n // PLANE, cols // PLANE
    rc = rows // n
    half = lanes // 2
    depth = slots * half
    x, y, z = m % 2, (m // 2) % 2, m // PLANE
    xy = m % PLANE
    base = m - xy
    o = (q + (z == 0).astype(jnp.int32)) % 2
    b1, b2 = x + o * (y - x), y + o * (x - y)
    w1, w2 = 1 + o, 2 - o
    partner1, partner2 = m + w1 * (1 - 2 * b1), m + w2 * (1 - 2 * b2)

    def remote(src, dst, send, recv, **where):
        return pltpu.make_async_remote_copy(
            src_ref=src, dst_ref=dst, send_sem=send, recv_sem=recv,
            device_id=where, device_id_type=MESH,
        )

    def tell(sem, **where):
        pl.semaphore_signal(sem, inc=1, device_id=where, device_id_type=MESH)

    def mate(d):
        return base + (xy + d) % PLANE

    def col_time(local, fin):
        return ((fin * cols + local) * width) // ncol

    def active(plane, g):
        return (plane * PLANE + PLANE) * slots - 1 >= col_time(g * PLANE, q)

    def column(g, flip1, flip2):
        c1 = 1 - b1 if flip1 else b1
        c2 = 1 - b2 if flip2 else b2
        return g * PLANE + c1 * w1 + c2 * w2

    order = []
    for flip1 in (True, False):
        for g in range(groups):
            order.append((column(g, flip1, True), column(g, flip1, False)))

    own_sigma = pltpu.make_async_copy(sigma_ref, sig.at[q], sig_local)
    own_sigma.start()
    own_prop = pltpu.make_async_copy(prop_hbm, prop_ref, prop_sem)
    own_prop.start()

    barrier = pltpu.get_barrier_semaphore()
    for d in range(1, f):
        tell(barrier, fin=(q + d) % f)
    for d in range(1, PLANE):
        tell(barrier, mid=mate(d))
    for p in range(1, planes):
        @pl.when(z < p)
        def _():
            tell(barrier, mid=p * PLANE + xy)

    def s_copies():
        return [
            pltpu.make_async_copy(
                sigma_ref.at[k, pl.ds(0, k)],
                sbuf.at[q, pl.ds(k * (k - 1) // 2, k)],
                s_local.at[k - 1],
            )
            for k in range(1, steps)
        ]

    @pl.when(m == 0)
    def _():
        for copy in s_copies():
            copy.start()

    loads = []
    for i, pair in enumerate(order):
        for j, c in enumerate(pair):
            copy = pltpu.make_async_copy(
                hist_ref.at[:, c], hist.at[c], hist_sem.at[2 * i + j]
            )
            loads.append(copy)
    for copy in loads[:2]:
        copy.start()

    def block_of(g, p):
        return outb.at[p, :, pl.ds(g * PLANE, PLANE)]

    zeros[...] = jnp.zeros_like(zeros)
    for g in range(groups):
        for p in range(planes):
            @pl.when(jnp.logical_not(active(p, g)))
            def _():
                pltpu.make_async_copy(zeros, block_of(g, p), o_recv.at[g, p]).start()

    def build(fq):
        lane = lax.broadcasted_iota(jnp.int32, (rf, lanes), 1)
        is_last = (m == n - 1).astype(F32)
        for k in range(steps):
            for t in range(slots // 2):
                a, b = sig[fq, k, 2 * t], sig[fq, k, 2 * t + 1]
                if 2 * t < k:
                    a = a * (m * slots + 2 * t >= k).astype(F32)
                if 2 * t + 1 < k:
                    b = b * (m * slots + 2 * t + 1 >= k).astype(F32)
                if k == 0 and 2 * t + 2 == slots:
                    b = b + prop_ref[pl.ds(pl.multiple_of(fq * rf, rf), rf)] * is_last
                real = jnp.where(lane < half, a, pltpu.roll(b, half, 1))
                imag = jnp.where(lane < half, pltpu.roll(a, half, 1), b)
                for part_id, value in enumerate((real, imag)):
                    row = (part_id * steps + k) * rf
                    high, low = split(value)
                    lhs[fq, row:row + rf, t * lanes:(t + 1) * lanes] = high
                    lhs[fq, row:row + rf, depth + t * lanes:depth + (t + 1) * lanes] = low

    own_sigma.wait()
    own_prop.wait()
    for copy in loads[2:]:
        copy.start()
    build(q)
    pl.semaphore_wait(barrier, f - 1 + PLANE - 1 + z)

    sig_out = []
    for d in range(1, f):
        copy = remote(sigma_ref, sig.at[q], sig_send.at[d], sig_recv.at[q], fin=(q + d) % f)
        copy.start()
        sig_out.append(copy)

    for d in range(1, PLANE):
        tell(greet, mid=mate(d))
    for p in range(planes - 1):
        @pl.when(z > p)
        def _():
            tell(greet, mid=p * PLANE + xy)

    pairs = sbuf.shape[1]
    chunks = range(pairs)

    def s_copy(to, slot, h):
        piece = sbuf.at[q, h]
        return remote(piece, piece, s_send.at[slot, h], s_recv.at[h], mid=to)

    def s_first(to, h):
        return s_copy(to, to, h)

    def s_second(p, h):
        return s_copy(p * PLANE + xy, PLANE + p, h)

    firsts = (2, 3, 1)

    @pl.when(m == 0)
    def _():
        for copy in s_copies():
            copy.wait()
        for h in chunks:
            for to in firsts:
                s_first(to, h).start()

    def prepare(i):
        for j, c in enumerate(order[i]):
            loads[2 * i + j].wait()

        @pl.when(active(z, i % groups))
        def _():
            for j, c in enumerate(order[i]):
                start = col_time(c, q)
                for s in range(slots):
                    keep = (m * slots + s >= start).astype(F32)
                    high, low = split(hist[c, s] * keep)
                    rhs[i, s * half:(s + 1) * half, j * lanes:(j + 1) * lanes] = high
                    rhs[i, depth + s * half:depth + (s + 1) * half, j * lanes:(j + 1) * lanes] = low

    def compute(i, fq):
        dot = functools.partial(jnp.dot, preferred_element_type=F32)
        total = dot(lhs[fq, :, :depth], rhs[i, :depth])
        total = total + dot(lhs[fq, :, :depth], rhs[i, depth:])
        total = total + dot(lhs[fq, :, depth:], rhs[i, :depth])
        many = steps * rf
        for j, c in enumerate(order[i]):
            block = total[:, j * lanes:(j + 1) * lanes]
            part[c, fq] = block[:many] + turn(block[many:])

    def x1_copy(g, j, fq):
        return remote(
            part.at[order[g][j], fq], rx1.at[g, j, fq],
            x1_send.at[g, j, fq], x1_recv.at[g, j, fq], mid=partner1,
        )

    def x2_copy(g, fq):
        return remote(
            part.at[order[groups + g][0], fq], rx2.at[g, fq],
            x2_send.at[g, fq], x2_recv.at[g, fq], mid=partner2,
        )

    def send(g, fq):
        @pl.when(active(z, g))
        def _():
            compute(g, fq)
            for j in range(2):
                x1_copy(g, j, fq).start()

    def hold(g, fq):
        @pl.when(active(z, g))
        def _():
            compute(groups + g, fq)

    def forward(g, fq):
        @pl.when(active(z, g))
        def _():
            c = order[groups + g][0]
            x1_copy(g, 0, fq).wait_recv()
            part[c, fq] = part[c, fq] + rx1[g, 0, fq]
            x2_copy(g, fq).start()

    for g in range(groups):
        prepare(g)
        send(g, q)
    others = [(q + r) % f for r in range(1, f)]
    for r, fq in enumerate(others):
        remote(sigma_ref, sig.at[fq], sig_send.at[1 + r], sig_recv.at[fq], fin=fq).wait_recv()
        build(fq)
        for g in range(groups):
            send(g, fq)

    pl.semaphore_wait(greet, PLANE - 1 + planes - 1 - z)

    @pl.when(z == 0)
    def _():
        for h in chunks:
            @pl.when(m != 0)
            def _():
                s_first(0, h).wait_recv()
            for p in reversed(range(planes // 2, planes)):
                s_second(p, h).start()
        for p in reversed(range(1, planes // 2)):
            for h in chunks:
                s_second(p, h).start()

    for g in range(groups):
        prepare(groups + g)
        for fq in (q, *others):
            hold(g, fq)
        for fq in (q, *others):
            forward(g, fq)

    @pl.when(z != 0)
    def _():
        for h in chunks:
            s_second(0, h).wait_recv()

    sx_out = []
    for d in range(1, f):
        copy = remote(sbuf.at[q], sbuf.at[q], sx_send.at[d], sx_recv.at[q], fin=(q + d) % f)
        copy.start()
        sx_out.append(copy)
    for fq in others:
        remote(sbuf.at[fq], sbuf.at[fq], sx_send.at[0], sx_recv.at[fq], fin=fq).wait_recv()

    dot = functools.partial(jnp.dot, preferred_element_type=F32)

    def exact(left, right):
        left_high, left_low = split(left)
        right_high, right_low = split(right)
        return dot(left_high, right_high) + dot(left_high, right_low) + dot(left_low, right_high)

    direct, whole = {}, {}
    for k in range(1, steps):
        for j in range(k):
            pieces = [sbuf[fq, k * (k - 1) // 2 + j] for fq in range(f)]
            block = jnp.concatenate(pieces, axis=0)
            direct[k, j] = block + prop_ref[...] if k == j + 1 else block
    for k in range(1, steps):
        for j in range(steps - 1):
            block = direct[k, j] if j < k else jnp.zeros((rows, lanes), F32)
            for i in range(j + 1, k):
                block = block + exact(direct[k, i], stack(whole[i, j]))
            whole[k, j] = block
            high, low = split(block)
            weights[0, (k - 1) * rows:k * rows, j * lanes:(j + 1) * lanes] = high
            weights[1, (k - 1) * rows:k * rows, j * lanes:(j + 1) * lanes] = low

    def o_copy(g, to):
        return remote(stage.at[g, to], outb.at[z, :, g * PLANE + xy], o_send.at[g], o_recv.at[g, z], mid=to)

    def finish(g):
        c = order[groups + g][1]
        row = []
        for fq in (q, *others):
            x1_copy(g, 1, fq).wait_recv()
            x2_copy(g, fq).wait_recv()
        for fq in range(f):
            part[c, fq] = part[c, fq] + rx1[g, 1, fq] + rx2[g, fq]
        for k in range(steps):
            pieces = [part[c, fq, k * rf:(k + 1) * rf] for fq in range(f)]
            row.append(jnp.concatenate(pieces, axis=0))
        high, low = split(jnp.concatenate([stack(row[k]) for k in range(steps - 1)], axis=0))
        dot = functools.partial(jnp.dot, preferred_element_type=F32)
        terms = dot(weights[0], high) + dot(weights[0], low) + dot(weights[1], high)
        for k in range(steps):
            value = row[k]
            if k > 0:
                value = value + terms[(k - 1) * rows:k * rows]
            for to in range(n):
                stage[g, to, k] = value[to * rc:(to + 1) * rc]
        hand(g, 0, near)

    def hand(g, first, last):
        for to in range(first, last):
            @pl.when(to != m)
            def _():
                o_copy(g, to).start()

    def own(g):
        pltpu.make_async_copy(stage.at[g, m], outb.at[z, :, g * PLANE + xy], o_recv.at[g, z]).start()

    near = PLANE
    for g in range(groups):
        @pl.when(active(z, g))
        def _():
            finish(g)

    for first in range(near, n, PLANE):
        for g in range(groups):
            @pl.when(active(z, g))
            def _():
                hand(g, first, first + PLANE)
    for g in range(groups):
        @pl.when(active(z, g))
        def _():
            own(g)

    for g in range(groups):
        for p in range(planes):
            pltpu.make_async_copy(block_of(g, p), block_of(g, p), o_recv.at[g, p]).wait()

    for copy in sig_out + sx_out:
        copy.wait_send()

    @pl.when(m == 0)
    def _():
        for h in chunks:
            for to in firsts:
                s_first(to, h).wait_send()

    @pl.when(z == 0)
    def _():
        for p in range(1, planes):
            for h in chunks:
                s_second(p, h).wait_send()

    for g in range(groups):
        @pl.when(active(z, g))
        def _():
            for fq in range(f):
                x1_copy(g, 0, fq).wait_send()
                x1_copy(g, 1, fq).wait_send()
                x2_copy(g, fq).wait_send()
            sent = stage.at[g, pl.ds(0, n - 1)]
            pltpu.make_async_copy(sent, sent, o_send.at[g]).wait()


def solution(mesh):
    n, f = mesh.shape["mid"], mesh.shape["fin"]

    def on_device(history, sigma, propagator):
        slots, cols, rows, lanes = history.shape
        steps, rf = sigma.shape[0], sigma.shape[2]
        rc, depth = rows // n, slots * lanes // 2
        planes, groups, pairs = n // PLANE, cols // PLANE, steps * (steps - 1) // 2
        many = steps * rf
        dma = pltpu.SemaphoreType.DMA
        anywhere = pl.BlockSpec(memory_space=pl.ANY)
        out = pl.pallas_call(
            functools.partial(kernel, n, f),
            out_shape=jax.ShapeDtypeStruct((planes, steps, cols, rc, lanes), F32),
            in_specs=[anywhere, anywhere, anywhere],
            out_specs=anywhere,
            scratch_shapes=[
                pltpu.VMEM((cols, slots, rows, lanes), F32),
                pltpu.VMEM((f, steps, slots, rf, lanes), F32),
                pltpu.VMEM((rows, lanes), F32),
                pltpu.VMEM((f, pairs, rf, lanes), F32),
                pltpu.VMEM((f, 2 * many, 2 * depth), BF16),
                pltpu.VMEM((2 * groups, 2 * depth, 2 * lanes), BF16),
                pltpu.VMEM((cols, f, many, lanes), F32),
                pltpu.VMEM((groups, 2, f, many, lanes), F32),
                pltpu.VMEM((groups, f, many, lanes), F32),
                pltpu.VMEM((2, (steps - 1) * rows, (steps - 1) * lanes), BF16),
                pltpu.VMEM((groups, n, steps, rc, lanes), F32),
                pltpu.VMEM((steps, PLANE, rc, lanes), F32),
                dma((cols,)), dma, dma, dma((f,)), dma((f,)),
                dma((steps - 1,)), dma((PLANE + planes, pairs)), dma((pairs,)),
                dma((f,)), dma((f,)), pltpu.SemaphoreType.REGULAR,
                dma((groups, 2, f)), dma((groups, 2, f)), dma((groups, f)), dma((groups, f)),
                dma((groups,)), dma((groups, planes)),
            ],
            compiler_params=pltpu.CompilerParams(
                collective_id=0, has_side_effects=True, vmem_limit_bytes=40 * 2**20
            ),
        )(*(pltpu.with_memory_space_constraint(a, pltpu.HBM) for a in (history, sigma, propagator)))
        return jnp.sum(out, axis=0)

    in_specs = (P("mid", "fin", None, None), P(None, "mid", "fin", None), P())
    return jax.shard_map(
        on_device, mesh=mesh, in_specs=in_specs, out_specs=P(None, "fin", "mid", None),
        check_vma=False,
    )
```

```python
import functools

import jax
import jax.numpy as jnp
from jax import lax
from jax.experimental import pallas as pl
from jax.experimental.pallas import tpu as pltpu
from jax.sharding import PartitionSpec as P

MESH = pl.DeviceIdType.MESH
PLANE = 4
F32 = jnp.float32
BF16 = jnp.bfloat16


def split(value):
    high = value.astype(BF16)
    return high, (value - high.astype(F32)).astype(BF16)


def turn(value):
    half = value.shape[-1] // 2
    rolled = pltpu.roll(value, half, 1)
    lane = lax.broadcasted_iota(jnp.int32, value.shape, 1)
    return jnp.where(lane < half, -rolled, rolled)


def stack(value):
    return jnp.concatenate([value, turn(value)], axis=0)


def kernel(
    n, f, hist_ref, sigma_ref, prop_hbm, outb,
    hist, sig, prop_ref, sbuf, lhs, rhs, part, rx1, rx2, weights, stage, zeros,
    hist_sem, prop_sem, sig_local, sig_send, sig_recv, s_local, s_send, s_recv,
    sx_send, sx_recv, greet, x1_send, x1_recv, x2_send, x2_recv, o_send, o_recv,
):
    m = lax.axis_index("mid")
    q = lax.axis_index("fin")
    slots, cols, rows, lanes = hist_ref.shape
    steps, rf = sigma_ref.shape[0], sigma_ref.shape[2]
    width, ncol = n * slots, f * cols
    planes, groups = n // PLANE, cols // PLANE
    rc = rows // n
    half = lanes // 2
    depth = slots * half
    x, y, z = m % 2, (m // 2) % 2, m // PLANE
    xy = m % PLANE
    base = m - xy
    o = (q + (z == 0).astype(jnp.int32)) % 2
    b1, b2 = x + o * (y - x), y + o * (x - y)
    w1, w2 = 1 + o, 2 - o
    partner1, partner2 = m + w1 * (1 - 2 * b1), m + w2 * (1 - 2 * b2)

    def remote(src, dst, send, recv, **where):
        return pltpu.make_async_remote_copy(
            src_ref=src, dst_ref=dst, send_sem=send, recv_sem=recv,
            device_id=where, device_id_type=MESH,
        )

    def tell(sem, **where):
        pl.semaphore_signal(sem, inc=1, device_id=where, device_id_type=MESH)

    def mate(d):
        return base + (xy + d) % PLANE

    def col_time(local, fin):
        return ((fin * cols + local) * width) // ncol

    def active(plane, g):
        return (plane * PLANE + PLANE) * slots - 1 >= col_time(g * PLANE, q)

    def column(g, flip1, flip2):
        c1 = 1 - b1 if flip1 else b1
        c2 = 1 - b2 if flip2 else b2
        return g * PLANE + c1 * w1 + c2 * w2

    order = []
    for flip1 in (True, False):
        for g in range(groups):
            order.append((column(g, flip1, True), column(g, flip1, False)))

    own_sigma = pltpu.make_async_copy(sigma_ref, sig.at[q], sig_local)
    own_sigma.start()
    own_prop = pltpu.make_async_copy(prop_hbm, prop_ref, prop_sem)
    own_prop.start()

    barrier = pltpu.get_barrier_semaphore()
    for d in range(1, f):
        tell(barrier, fin=(q + d) % f)
    for d in range(1, PLANE):
        tell(barrier, mid=mate(d))
    for p in range(1, planes):
        @pl.when(z < p)
        def _():
            tell(barrier, mid=p * PLANE + xy)

    def s_copies():
        return [
            pltpu.make_async_copy(
                sigma_ref.at[k, pl.ds(0, k)],
                sbuf.at[q, pl.ds(k * (k - 1) // 2, k)],
                s_local.at[k - 1],
            )
            for k in range(1, steps)
        ]

    @pl.when(m == 0)
    def _():
        for copy in s_copies():
            copy.start()

    loads = []
    for i, pair in enumerate(order):
        for j, c in enumerate(pair):
            copy = pltpu.make_async_copy(
                hist_ref.at[:, c], hist.at[c], hist_sem.at[2 * i + j]
            )
            loads.append(copy)
    for copy in loads:
        copy.start()

    def block_of(g, p):
        return outb.at[p, :, pl.ds(g * PLANE, PLANE)]

    zeros[...] = jnp.zeros_like(zeros)
    for g in range(groups):
        for p in range(planes):
            @pl.when(jnp.logical_not(active(p, g)))
            def _():
                pltpu.make_async_copy(zeros, block_of(g, p), o_recv.at[g, p]).start()

    def build(fq):
        lane = lax.broadcasted_iota(jnp.int32, (rf, lanes), 1)
        is_last = (m == n - 1).astype(F32)
        for k in range(steps):
            for t in range(slots // 2):
                a, b = sig[fq, k, 2 * t], sig[fq, k, 2 * t + 1]
                if 2 * t < k:
                    a = a * (m * slots + 2 * t >= k).astype(F32)
                if 2 * t + 1 < k:
                    b = b * (m * slots + 2 * t + 1 >= k).astype(F32)
                if k == 0 and 2 * t + 2 == slots:
                    b = b + prop_ref[pl.ds(pl.multiple_of(fq * rf, rf), rf)] * is_last
                real = jnp.where(lane < half, a, pltpu.roll(b, half, 1))
                imag = jnp.where(lane < half, pltpu.roll(a, half, 1), b)
                for part_id, value in enumerate((real, imag)):
                    row = (part_id * steps + k) * rf
                    high, low = split(value)
                    lhs[fq, row:row + rf, t * lanes:(t + 1) * lanes] = high
                    lhs[fq, row:row + rf, depth + t * lanes:depth + (t + 1) * lanes] = low

    own_sigma.wait()
    own_prop.wait()
    build(q)
    pl.semaphore_wait(barrier, f - 1 + PLANE - 1 + z)

    sig_out = []
    for d in range(1, f):
        copy = remote(sigma_ref, sig.at[q], sig_send.at[d], sig_recv.at[q], fin=(q + d) % f)
        copy.start()
        sig_out.append(copy)

    for d in range(1, PLANE):
        tell(greet, mid=mate(d))
    for p in range(planes - 1):
        @pl.when(z > p)
        def _():
            tell(greet, mid=p * PLANE + xy)

    pairs = sbuf.shape[1]
    chunks = range(pairs)

    def s_copy(to, slot, h):
        piece = sbuf.at[q, h]
        return remote(piece, piece, s_send.at[slot, h], s_recv.at[h], mid=to)

    def s_first(to, h):
        return s_copy(to, to, h)

    def s_second(p, h):
        return s_copy(p * PLANE + xy, PLANE + p, h)

    firsts = (2, 3, 1)

    @pl.when(m == 0)
    def _():
        for copy in s_copies():
            copy.wait()
        for h in chunks:
            for to in firsts:
                s_first(to, h).start()

    def prepare(i):
        for j, c in enumerate(order[i]):
            loads[2 * i + j].wait()

        @pl.when(active(z, i % groups))
        def _():
            for j, c in enumerate(order[i]):
                start = col_time(c, q)
                for s in range(slots):
                    keep = (m * slots + s >= start).astype(F32)
                    high, low = split(hist[c, s] * keep)
                    rhs[i, s * half:(s + 1) * half, j * lanes:(j + 1) * lanes] = high
                    rhs[i, depth + s * half:depth + (s + 1) * half, j * lanes:(j + 1) * lanes] = low

    def compute(i, fq):
        dot = functools.partial(jnp.dot, preferred_element_type=F32)
        total = dot(lhs[fq, :, :depth], rhs[i, :depth])
        total = total + dot(lhs[fq, :, :depth], rhs[i, depth:])
        total = total + dot(lhs[fq, :, depth:], rhs[i, :depth])
        many = steps * rf
        for j, c in enumerate(order[i]):
            block = total[:, j * lanes:(j + 1) * lanes]
            part[c, fq] = block[:many] + turn(block[many:])

    def x1_copy(g, j, fq):
        return remote(
            part.at[order[g][j], fq], rx1.at[g, j, fq],
            x1_send.at[g, j, fq], x1_recv.at[g, j, fq], mid=partner1,
        )

    def x2_copy(g, fq):
        return remote(
            part.at[order[groups + g][0], fq], rx2.at[g, fq],
            x2_send.at[g, fq], x2_recv.at[g, fq], mid=partner2,
        )

    def send(g, fq):
        @pl.when(active(z, g))
        def _():
            compute(g, fq)
            for j in range(2):
                x1_copy(g, j, fq).start()

    def hold(g, fq):
        @pl.when(active(z, g))
        def _():
            compute(groups + g, fq)

    def forward(g, fq):
        @pl.when(active(z, g))
        def _():
            c = order[groups + g][0]
            x1_copy(g, 0, fq).wait_recv()
            part[c, fq] = part[c, fq] + rx1[g, 0, fq]
            x2_copy(g, fq).start()

    for g in range(groups):
        prepare(g)
        send(g, q)
    others = [(q + r) % f for r in range(1, f)]
    for r, fq in enumerate(others):
        remote(sigma_ref, sig.at[fq], sig_send.at[1 + r], sig_recv.at[fq], fin=fq).wait_recv()
        build(fq)
        for g in range(groups):
            send(g, fq)

    pl.semaphore_wait(greet, PLANE - 1 + planes - 1 - z)

    @pl.when(z == 0)
    def _():
        for h in chunks:
            @pl.when(m != 0)
            def _():
                s_first(0, h).wait_recv()
            for p in reversed(range(planes // 2, planes)):
                s_second(p, h).start()
        for p in reversed(range(1, planes // 2)):
            for h in chunks:
                s_second(p, h).start()

    for g in range(groups):
        prepare(groups + g)
        for fq in (q, *others):
            hold(g, fq)
        for fq in (q, *others):
            forward(g, fq)

    @pl.when(z != 0)
    def _():
        for h in chunks:
            s_second(0, h).wait_recv()

    sx_out = []
    for d in range(1, f):
        copy = remote(sbuf.at[q], sbuf.at[q], sx_send.at[d], sx_recv.at[q], fin=(q + d) % f)
        copy.start()
        sx_out.append(copy)
    for fq in others:
        remote(sbuf.at[fq], sbuf.at[fq], sx_send.at[0], sx_recv.at[fq], fin=fq).wait_recv()

    dot = functools.partial(jnp.dot, preferred_element_type=F32)

    def exact(left, right):
        left_high, left_low = split(left)
        right_high, right_low = split(right)
        return dot(left_high, right_high) + dot(left_high, right_low) + dot(left_low, right_high)

    direct, whole = {}, {}
    for k in range(1, steps):
        for j in range(k):
            pieces = [sbuf[fq, k * (k - 1) // 2 + j] for fq in range(f)]
            block = jnp.concatenate(pieces, axis=0)
            direct[k, j] = block + prop_ref[...] if k == j + 1 else block
    for k in range(1, steps):
        for j in range(steps - 1):
            block = direct[k, j] if j < k else jnp.zeros((rows, lanes), F32)
            for i in range(j + 1, k):
                block = block + exact(direct[k, i], stack(whole[i, j]))
            whole[k, j] = block
            high, low = split(block)
            weights[0, (k - 1) * rows:k * rows, j * lanes:(j + 1) * lanes] = high
            weights[1, (k - 1) * rows:k * rows, j * lanes:(j + 1) * lanes] = low

    def o_copy(g, to):
        return remote(stage.at[g, to], outb.at[z, :, g * PLANE + xy], o_send.at[g], o_recv.at[g, z], mid=to)

    def finish(g):
        c = order[groups + g][1]
        row = []
        for fq in (q, *others):
            x1_copy(g, 1, fq).wait_recv()
            x2_copy(g, fq).wait_recv()
        for fq in range(f):
            part[c, fq] = part[c, fq] + rx1[g, 1, fq] + rx2[g, fq]
        for k in range(steps):
            pieces = [part[c, fq, k * rf:(k + 1) * rf] for fq in range(f)]
            row.append(jnp.concatenate(pieces, axis=0))
        high, low = split(jnp.concatenate([stack(row[k]) for k in range(steps - 1)], axis=0))
        dot = functools.partial(jnp.dot, preferred_element_type=F32)
        terms = dot(weights[0], high) + dot(weights[0], low) + dot(weights[1], high)
        for k in range(steps):
            value = row[k]
            if k > 0:
                value = value + terms[(k - 1) * rows:k * rows]
            for to in range(n):
                stage[g, to, k] = value[to * rc:(to + 1) * rc]
        for to in range(n):
            @pl.when(to != m)
            def _():
                o_copy(g, to).start()
        pltpu.make_async_copy(stage.at[g, m], outb.at[z, :, g * PLANE + xy], o_recv.at[g, z]).start()

    for g in range(groups):
        @pl.when(active(z, g))
        def _():
            finish(g)

    for g in range(groups):
        for p in range(planes):
            pltpu.make_async_copy(block_of(g, p), block_of(g, p), o_recv.at[g, p]).wait()

    for copy in sig_out + sx_out:
        copy.wait_send()

    @pl.when(m == 0)
    def _():
        for h in chunks:
            for to in firsts:
                s_first(to, h).wait_send()

    @pl.when(z == 0)
    def _():
        for p in range(1, planes):
            for h in chunks:
                s_second(p, h).wait_send()

    for g in range(groups):
        @pl.when(active(z, g))
        def _():
            for fq in range(f):
                x1_copy(g, 0, fq).wait_send()
                x1_copy(g, 1, fq).wait_send()
                x2_copy(g, fq).wait_send()
            sent = stage.at[g, pl.ds(0, n - 1)]
            pltpu.make_async_copy(sent, sent, o_send.at[g]).wait()


def solution(mesh):
    n, f = mesh.shape["mid"], mesh.shape["fin"]

    def on_device(history, sigma, propagator):
        slots, cols, rows, lanes = history.shape
        steps, rf = sigma.shape[0], sigma.shape[2]
        rc, depth = rows // n, slots * lanes // 2
        planes, groups, pairs = n // PLANE, cols // PLANE, steps * (steps - 1) // 2
        many = steps * rf
        dma = pltpu.SemaphoreType.DMA
        anywhere = pl.BlockSpec(memory_space=pl.ANY)
        out = pl.pallas_call(
            functools.partial(kernel, n, f),
            out_shape=jax.ShapeDtypeStruct((planes, steps, cols, rc, lanes), F32),
            in_specs=[anywhere, anywhere, anywhere],
            out_specs=anywhere,
            scratch_shapes=[
                pltpu.VMEM((cols, slots, rows, lanes), F32),
                pltpu.VMEM((f, steps, slots, rf, lanes), F32),
                pltpu.VMEM((rows, lanes), F32),
                pltpu.VMEM((f, pairs, rf, lanes), F32),
                pltpu.VMEM((f, 2 * many, 2 * depth), BF16),
                pltpu.VMEM((2 * groups, 2 * depth, 2 * lanes), BF16),
                pltpu.VMEM((cols, f, many, lanes), F32),
                pltpu.VMEM((groups, 2, f, many, lanes), F32),
                pltpu.VMEM((groups, f, many, lanes), F32),
                pltpu.VMEM((2, (steps - 1) * rows, (steps - 1) * lanes), BF16),
                pltpu.VMEM((groups, n, steps, rc, lanes), F32),
                pltpu.VMEM((steps, PLANE, rc, lanes), F32),
                dma((cols,)), dma, dma, dma((f,)), dma((f,)),
                dma((steps - 1,)), dma((PLANE + planes, pairs)), dma((pairs,)),
                dma((f,)), dma((f,)), pltpu.SemaphoreType.REGULAR,
                dma((groups, 2, f)), dma((groups, 2, f)), dma((groups, f)), dma((groups, f)),
                dma((groups,)), dma((groups, planes)),
            ],
            compiler_params=pltpu.CompilerParams(
                collective_id=0, has_side_effects=True, vmem_limit_bytes=40 * 2**20
            ),
        )(*(pltpu.with_memory_space_constraint(a, pltpu.HBM) for a in (history, sigma, propagator)))
        return jnp.sum(out, axis=0)

    in_specs = (P("mid", "fin", None, None), P(None, "mid", "fin", None), P())
    return jax.shard_map(
        on_device, mesh=mesh, in_specs=in_specs, out_specs=P(None, "fin", "mid", None),
        check_vma=False,
    )
```
